32 devices in a mesh: groups: 2 (over y), ctx: 4 (over z), section: 2 (over x), head: 2 (over core).
Axes of the slice: x: 2, y: 2, z: 4, core: 2. Of those that a mesh axis runs over, the one named last changes fastest.
Arguments:
- tokens: bfloat16 [4, 512, 2048], P('groups', 'ctx', 'head'), parts along dimension 0, may hold values from -20 to 20
- norm_gain: bfloat16 [2, 2048], P('section'), may hold values from 0.5 to 1.5
- w_query: bfloat16 [2, 2048, 256], P('section', None, 'head'), may hold values from -0.125 to 0.125
- w_key: bfloat16 [2, 2048, 256], P('section', None, 'head'), may hold values from -0.125 to 0.125
- w_value: bfloat16 [2, 2048, 2048], P('section', None, 'head'), may hold values from -0.125 to 0.125
- conv_query: bfloat16 [2, 4, 256], P('section', None, 'head'), may hold values from -3 to 3
- conv_key: bfloat16 [2, 4, 256], P('section', None, 'head'), may hold values from -3 to 3
- conv_value: bfloat16 [2, 4, 2048], P('section', None, 'head'), may hold values from -3 to 3
- value_gain: bfloat16 [2, 2048], P('section', 'head'), may hold values from 0.5 to 1.5
- w_out: bfloat16 [2, 2048, 2048], P('section', 'head'), may hold values from -0.125 to 0.125
- doc_start: int32 [4], P('groups'), parts along dimension 0, may hold values from 1 to 511
- pad_length: int32 [4], P('groups'), parts along dimension 0, may hold values from 0 to 255
Outputs:
- layer_outputs: bfloat16 [2, 4, 512, 2048], P('section', 'groups', 'ctx', 'head'), parts along dimension 1
The draws below stay inside these ranges and needn't reach their ends.
There are 2 independent parts, one for each index of `groups`. The reference program is written for one: setup_inputs(seed, part) draws one part's arguments, and reference() takes and returns one part's arrays. A program takes and returns all parts, laid end to end along the dimension named above; an argument that names none is the same for every part. Nothing has to cross between parts.
All inputs are finite; a program needn't handle non-finite values.
Results may differ from the reference program's by a relative error of at most 0.0061.
Values may be sent and summed in bfloat16 or wider, within the bound.
A program may use at most 128 MiB of HBM per device.

```python
import math
import jax
import jax.numpy as jnp
import numpy as np
from jax import lax

D = 2048
HEADS = 16
FD = 16
HD = 128
FEAT = 153
KCONV = 4
SPAN = 128
MICRO = 2
WINDOW = 512
LAYERS = 2


def draw_tokens(key, part):
    key_rows, key_cols, key_main = jax.random.split(key, 3)
    row_scale = jnp.exp(jax.random.uniform(key_rows, (MICRO, WINDOW, 1), jnp.float32, math.log(0.7), math.log(1.4)))
    col_scale = jnp.exp(jax.random.uniform(key_cols, (1, 1, D), jnp.float32, math.log(0.35), math.log(3.5)))
    values = jnp.clip(jax.random.normal(key_main, (MICRO, WINDOW, D), jnp.float32), -4.0, 4.0)
    return (values * row_scale * col_scale).astype(jnp.bfloat16)


def steps_of(own_key, shape, cuts, smallest, top_value):
    def one(position, parts):
        steps = jax.random.uniform(jax.random.fold_in(jax.random.fold_in(own_key, 6), position), (parts,), jnp.float32, smallest / len(cuts), top_value / len(cuts))
        return jnp.repeat(jnp.exp(steps), shape[position] // parts).reshape((-1,) + (1,) * (len(shape) - position - 1))

    factor_of = one(*cuts[0])
    for cut in cuts[1:]:
        factor_of = factor_of * one(*cut)
    return factor_of


def bell_draw(rng, dims, deviation, most, cuts=(), kind=jnp.bfloat16):
    entries = jax.random.normal(rng, dims, jnp.float32) * deviation
    if len(cuts) > 0:
        entries = steps_of(rng, dims, cuts, -0.22, 0.18) * entries
    return jnp.clip(entries, min=-most, max=most).astype(kind)


def setup_inputs(seed: int = 0, part: int = 0) -> dict:
    key_list = jax.random.split(jax.random.key(seed), 13)
    part_splits = jax.random.split(jax.random.fold_in(key_list[12], part), 13)
    tokens = draw_tokens(jax.random.fold_in(jax.random.fold_in(key_list[12], part), 71), part)
    norm_gain = jnp.clip(1.0 + 0.1 * jax.random.normal(key_list[1], (LAYERS, D), jnp.float32), 0.5, 1.5).astype(jnp.bfloat16)
    w_query = bell_draw(key_list[2], (LAYERS, D, HEADS * FD), D ** -0.5, 0.125, ((0, 2), (2, 2)))
    w_key = bell_draw(key_list[3], (LAYERS, D, HEADS * FD), D ** -0.5, 0.125, ((0, 2), (2, 2)))
    w_value = bell_draw(key_list[4], (LAYERS, D, HEADS * HD), D ** -0.5, 0.125, ((0, 2), (2, 2)))
    conv_query = bell_draw(key_list[5], (LAYERS, KCONV, HEADS * FD), KCONV ** -0.5, 3.0, ((0, 2), (2, 2)))
    conv_key = bell_draw(key_list[6], (LAYERS, KCONV, HEADS * FD), KCONV ** -0.5, 3.0, ((0, 2), (2, 2)))
    conv_value = bell_draw(key_list[7], (LAYERS, KCONV, HEADS * HD), KCONV ** -0.5, 3.0, ((0, 2), (2, 2)))
    value_gain = jnp.clip(1.0 + 0.1 * jax.random.normal(key_list[8], (LAYERS, HEADS * HD), jnp.float32), 0.5, 1.5).astype(jnp.bfloat16)
    w_out = bell_draw(key_list[9], (LAYERS, HEADS * HD, D), (HEADS * HD) ** -0.5, 0.125, ((0, 2), (1, 2)))
    doc_start = jax.random.randint(part_splits[10], (MICRO,), 1, WINDOW).astype(jnp.int32)
    pad_length = jax.random.randint(part_splits[11], (MICRO,), 0, 2 * SPAN).astype(jnp.int32)
    return dict(tokens=tokens, norm_gain=norm_gain, w_query=w_query, w_key=w_key, w_value=w_value, conv_query=conv_query, conv_key=conv_key, conv_value=conv_value, value_gain=value_gain, w_out=w_out, doc_start=doc_start, pad_length=pad_length)


norm_eps = 1e-06

def pair_tables(feat_width):
    left_list = []
    right_list = []
    weight_list = []
    for left_pos in range(feat_width):
        for right_pos in range(left_pos, feat_width):
            left_list.append(left_pos)
            right_list.append(right_pos)
            if left_pos == right_pos:
                weight_list.append(1.0 / math.sqrt(2.0 * feat_width))
            else:
                weight_list.append(1.0 / math.sqrt(feat_width))
    return (np.array(left_list, np.int32), np.array(right_list, np.int32), weight_list)

def taylor_features(vectors):
    feat_width = vectors.shape[-1]
    left_index, right_index, weight_list = pair_tables(feat_width)
    pair_weight = jnp.asarray(weight_list, dtype=jnp.float32)
    constant = jnp.ones(vectors.shape[:-1] + (1,), jnp.float32)
    linear = vectors * (1.0 / feat_width ** 0.25)
    quadratic = vectors[..., left_index] * vectors[..., right_index] * pair_weight
    return jnp.concatenate([constant, linear, quadratic], axis=-1)

def normed_rows(hidden, gain):
    row_values = hidden.astype(jnp.float32)
    mean_square = lax.optimization_barrier(jnp.mean(row_values * row_values, axis=-1, keepdims=True))
    return (row_values * lax.rsqrt(mean_square + norm_eps) * gain.astype(jnp.float32)).astype(jnp.bfloat16)

def short_conv(extended, tap_weights, positions, boundary):
    tap_count = tap_weights.shape[0]
    row_count = extended.shape[0] - tap_count + 1
    summed = jnp.zeros((row_count, extended.shape[1]), jnp.float32)
    after_start = positions >= boundary
    for offset in range(tap_count):
        source = extended[tap_count - 1 - offset:tap_count - 1 - offset + row_count].astype(jnp.float32)
        earlier_side = positions - offset >= boundary
        keep_rows = (earlier_side == after_start).astype(jnp.float32)
        summed = summed + tap_weights[offset].astype(jnp.float32) * source * keep_rows[:, None]
    return summed

def mix_rows(queries, key_vals, values, positions, boundary, carried, value_gain):
    row_count = queries.shape[0]
    head_count = values.shape[1] // HD
    query_heads = queries.reshape(row_count, head_count, -1)
    key_heads = key_vals.reshape(row_count, head_count, -1)
    value_heads = values.reshape(row_count, head_count, HD)
    feat_width = query_heads.shape[-1]
    scores = jnp.einsum('ihd,jhd->hij', query_heads, key_heads, precision=lax.Precision.HIGHEST) / math.sqrt(feat_width)
    after_start = positions >= boundary
    allowed = (positions[None, :] <= positions[:, None]) & (after_start[None, :] == after_start[:, None])
    weights = jnp.where(allowed[None], 1.0 + scores + 0.5 * scores * scores, 0.0).astype(jnp.bfloat16)
    local_part = jnp.einsum('hij,jhd->ihd', weights.astype(jnp.float32), value_heads.astype(jnp.float32))
    block_start = positions[0]
    use_carried = (positions < boundary) | (boundary < block_start)
    query_feats = taylor_features(query_heads)
    far_part = jnp.einsum('ihf,hfd->ihd', query_feats, carried, precision=lax.Precision.HIGHEST)
    far_part = far_part * use_carried.astype(jnp.float32)[:, None, None]
    numerator = local_part + far_part
    mean_square = lax.optimization_barrier(jnp.mean(numerator * numerator, axis=-1, keepdims=True))
    scaled = numerator * lax.rsqrt(mean_square + norm_eps)
    return (scaled.reshape(row_count, -1) * value_gain.astype(jnp.float32)).astype(jnp.bfloat16)

def local_state(key_vals, values, positions, boundary):
    row_count = key_vals.shape[0]
    head_count = values.shape[1] // HD
    key_heads = key_vals.reshape(row_count, head_count, -1)
    value_heads = values.reshape(row_count, head_count, HD)
    block_start = positions[0]
    reset_here = (boundary >= block_start) & (boundary < block_start + row_count)
    keep_keys = (positions >= boundary) | jnp.logical_not(reset_here)
    key_feats = (taylor_features(key_heads) * keep_keys.astype(jnp.float32)[:, None, None]).astype(jnp.bfloat16)
    block_state = jnp.einsum('jhf,jhd->hfd', key_feats.astype(jnp.float32), value_heads.astype(jnp.float32))
    return (block_state, reset_here)

def apply_layer(hidden, gain_norm, weight_query, weight_key, weight_value, taps_query, taps_key, taps_value, gain_value, weight_out, boundary, pad_count):
    window_rows = hidden.shape[0]
    positions = jnp.arange(window_rows, dtype=jnp.int32)
    normed = normed_rows(hidden, gain_norm)
    rim_rows = taps_query.shape[0] - 1

    def project_conv(weight_matrix, tap_weights):
        projected_rows = jnp.dot(normed, weight_matrix, preferred_element_type=jnp.float32).astype(jnp.bfloat16)
        extended = jnp.concatenate([jnp.zeros((rim_rows, projected_rows.shape[1]), jnp.bfloat16), projected_rows], axis=0)
        return short_conv(extended, tap_weights, positions, boundary)
    queries = project_conv(weight_query, taps_query)
    key_vals = project_conv(weight_key, taps_key)
    values = project_conv(weight_value, taps_value).astype(jnp.bfloat16)
    block_count = window_rows // SPAN

    def step_block(carried, block_pos):
        first_row = (block_pos * SPAN).astype(jnp.int32)
        block_queries = lax.dynamic_slice_in_dim(queries, first_row, SPAN, 0)
        block_keys = lax.dynamic_slice_in_dim(key_vals, first_row, SPAN, 0)
        block_values = lax.dynamic_slice_in_dim(values, first_row, SPAN, 0)
        block_positions = first_row + jnp.arange(SPAN, dtype=jnp.int32)
        mixed_rows = mix_rows(block_queries, block_keys, block_values, block_positions, boundary, carried, gain_value)
        block_state, reset_here = local_state(block_keys, block_values, block_positions, boundary)
        next_state = block_state + jnp.where(reset_here, 0.0, 1.0) * carried
        return (next_state, mixed_rows)
    start_state = jnp.zeros((HEADS, FEAT, HD), jnp.float32)
    final_state, mixed_blocks = lax.scan(step_block, start_state, jnp.arange(block_count, dtype=jnp.int32))
    mixed_all = mixed_blocks.reshape(window_rows, -1)
    update = jnp.dot(mixed_all, weight_out, preferred_element_type=jnp.float32)
    valid_rows = (positions < window_rows - pad_count).astype(jnp.float32)[:, None]
    return (hidden.astype(jnp.float32) + update * valid_rows).astype(jnp.bfloat16)

def reference(tokens, norm_gain, w_query, w_key, w_value, conv_query, conv_key, conv_value, value_gain, w_out, doc_start, pad_length):
    results = []
    for layer_pos in range(LAYERS):
        layer_rows_out = []
        for micro_pos in range(MICRO):
            if layer_pos == 0:
                hidden = tokens[micro_pos]
            else:
                hidden = results[layer_pos - 1][micro_pos]
            layer_rows_out.append(apply_layer(hidden, norm_gain[layer_pos], w_query[layer_pos], w_key[layer_pos], w_value[layer_pos], conv_query[layer_pos], conv_key[layer_pos], conv_value[layer_pos], value_gain[layer_pos], w_out[layer_pos], doc_start[micro_pos], pad_length[micro_pos]))
        results.append(jnp.stack(layer_rows_out))
    return jnp.stack(results)
```

```python
import math

import jax
import jax.numpy as jnp
from jax import lax
from jax.experimental import pallas as pl
from jax.experimental.pallas import tpu as pltpu
from jax.sharding import PartitionSpec as P

HD = 128
FD = 16
FROWS = 160
CHUNK = 256
EPS = 1e-06
MESH = pl.DeviceIdType.MESH
F32 = jnp.float32
BF16 = jnp.bfloat16


def features(doubled, first):
    x = doubled[first + (pl.ds(0, FD), slice(None))]
    rows = [x * (1.0 / FD**0.25), x * x * (1.0 / math.sqrt(2.0 * FD))]
    for d in range(1, FD // 2):
        rows.append(x * doubled[first + (pl.ds(d, FD), slice(None))] * (1.0 / math.sqrt(FD)))
    half = FD // 2
    rows.append(x[:half] * x[half:] * (1.0 / math.sqrt(FD)))
    lead = lax.broadcasted_iota(jnp.int32, (half, x.shape[1]), 0) == 0
    rows.append(jnp.where(lead, 1.0, 0.0))
    return jnp.concatenate(rows, axis=0)


def make_kernel(sizes):
    ctx_n, sec_n, windows, span, width, taps = sizes
    half = width // 2
    rows_n = windows * span
    heads = half // HD
    vchunks = half // CHUNK
    hop_lag = 2
    steps = heads + hop_lag * max(ctx_n - 2, 0)

    def kernel(
        start_ref, pad_ref, tok_ref, gain_ref, wq_ref, wk_ref, wv_ref, cq_ref, ck_ref, cv_ref, vg_ref, wo_ref,
        out_ref,
        w_all, wo_v, x_ref, n_ref, pr_ref, q3_ref, k3_ref, qt_ref, kt_ref, v_ref, bs_ref, got_ref, fwd_ref,
        num_ref, mix_ref, part_ref, other_ref,
        w_sem, x_send, x_recv, sec_send, sec_recv, halo_send, halo_recv, st_send, st_recv, p_send, p_recv,
    ):
        ctx = lax.axis_index("ctx")
        sec = lax.axis_index("section")
        core = lax.axis_index("head")
        mate = 1 - core

        loads = [
            pltpu.make_async_copy(wq_ref.at[0], w_all.at[:, pl.ds(0, HD)], w_sem.at[0]),
            pltpu.make_async_copy(wk_ref.at[0], w_all.at[:, pl.ds(HD, HD)], w_sem.at[1]),
        ]
        for j in range(vchunks):
            loads.append(
                pltpu.make_async_copy(
                    wv_ref.at[0, :, pl.ds(j * CHUNK, CHUNK)],
                    w_all.at[:, pl.ds((j + 1) * CHUNK, CHUNK)],
                    w_sem.at[2 + j],
                )
            )
        wo_load = pltpu.make_async_copy(wo_ref.at[0], wo_v, w_sem.at[2 + vchunks])
        for load in loads:
            load.start()
        wo_load.start()

        barrier = pltpu.get_barrier_semaphore()
        pl.semaphore_signal(barrier, inc=1, device_id={"head": mate}, device_id_type=MESH)

        @pl.when(ctx > 0)
        def _():
            pl.semaphore_signal(barrier, inc=1, device_id={"ctx": ctx - 1}, device_id_type=MESH)

        @pl.when(ctx < ctx_n - 1)
        def _():
            pl.semaphore_signal(barrier, inc=1, device_id={"ctx": ctx + 1}, device_id_type=MESH)

        @pl.when(sec > 0)
        def _():
            pl.semaphore_signal(barrier, inc=1, device_id={"section": sec - 1}, device_id_type=MESH)

        @pl.when(sec < sec_n - 1)
        def _():
            pl.semaphore_signal(barrier, inc=1, device_id={"section": sec + 1}, device_id_type=MESH)

        peers = (
            1
            + jnp.where(ctx > 0, 1, 0)
            + jnp.where(ctx < ctx_n - 1, 1, 0)
            + jnp.where(sec > 0, 1, 0)
            + jnp.where(sec < sec_n - 1, 1, 0)
        )
        pl.semaphore_wait(barrier, peers)

        def cols(j):
            return pl.ds(j * CHUNK, CHUNK)

        def section_copy(j):
            return pltpu.make_async_remote_copy(
                src_ref=out_ref.at[:, cols(j)],
                dst_ref=x_ref.at[core, :, cols(j)],
                send_sem=sec_send.at[j],
                recv_sem=sec_recv.at[j],
                device_id={"section": sec + 1},
                device_id_type=MESH,
            )

        def mate_copy(j):
            return pltpu.make_async_remote_copy(
                src_ref=x_ref.at[core, :, cols(j)],
                dst_ref=x_ref.at[core, :, cols(j)],
                send_sem=x_send.at[j],
                recv_sem=x_recv.at[j],
                device_id={"head": mate},
                device_id_type=MESH,
            )

        @pl.when(sec == 0)
        def _():
            x_ref[core] = tok_ref[...]

        for j in range(vchunks):

            @pl.when(sec > 0)
            def _():
                section_copy(j).wait_recv()

            mate_copy(j).start()

        first = ctx * span
        col_pos = first + lax.broadcasted_iota(jnp.int32, (span, HD), 0)
        lane_pos = first + lax.broadcasted_iota(jnp.int32, (1, span), 1)
        starts = [start_ref[m] for m in range(windows)]

        for j in range(vchunks):
            mate_copy(j).wait_recv()

        block = 32

        def norm_rows(i, carry):
            at = pl.ds(pl.multiple_of(i * block, block), block)
            left = x_ref[0, at, :].astype(F32)
            right = x_ref[1, at, :].astype(F32)
            square = jnp.sum(left * left, axis=1, keepdims=True) + jnp.sum(right * right, axis=1, keepdims=True)
            scale = lax.rsqrt(square * (1.0 / width) + EPS)
            n_ref[at, pl.ds(0, half)] = (left * scale * gain_ref[:, pl.ds(0, half)].astype(F32)).astype(BF16)
            n_ref[at, pl.ds(half, half)] = (right * scale * gain_ref[:, pl.ds(half, half)].astype(F32)).astype(BF16)
            return carry

        lax.fori_loop(0, rows_n // block, norm_rows, 0)

        def halo_copy(j):
            return pltpu.make_async_remote_copy(
                src_ref=pr_ref.at[:, pl.ds(span, 8), cols(j)],
                dst_ref=pr_ref.at[:, pl.ds(0, 8), cols(j)],
                send_sem=halo_send.at[j],
                recv_sem=halo_recv.at[j],
                device_id={"ctx": ctx + 1},
                device_id_type=MESH,
            )

        @pl.when(ctx == 0)
        def _():
            pr_ref[:, pl.ds(0, 8), :] = jnp.zeros((windows, 8, half + CHUNK), F32)

        for j in range(vchunks + 1):
            if j == 0:
                loads[0].wait()
                loads[1].wait()
            else:
                loads[1 + j].wait()
            got = jnp.dot(n_ref[...], w_all[:, cols(j)], preferred_element_type=F32).astype(BF16).astype(F32)
            for m in range(windows):
                pr_ref[m, pl.ds(8, span), cols(j)] = got[m * span : (m + 1) * span]

            @pl.when(ctx < ctx_n - 1)
            def _():
                halo_copy(j).start()

        def conv(m, at, taps_ref, tap_at):
            after = col_pos >= starts[m]
            total = None
            for j in range(taps):
                source = pr_ref[m, pl.ds(8 - j, span), at]
                term = taps_ref[0, pl.ds(j, 1), tap_at].astype(F32) * source
                if j:
                    same = (col_pos - j >= starts[m]) == after
                    term = jnp.where(same, term, 0.0)
                total = term if total is None else total + term
            return total

        def halo_wait(j):
            @pl.when(ctx > 0)
            def _():
                halo_copy(j).wait_recv()

        halo_wait(0)
        for m in range(windows):
            for which, taps_ref, wide_ref, turned_ref in ((0, cq_ref, q3_ref, qt_ref), (1, ck_ref, k3_ref, kt_ref)):
                part = conv(m, pl.ds(which * HD, HD), taps_ref, pl.ds(0, HD))
                high = part.astype(BF16)
                low = (part - high.astype(F32)).astype(BF16)
                wide_ref[m, :, pl.ds(0, HD)] = high
                wide_ref[m, :, pl.ds(HD, HD)] = high if which == 0 else low
                wide_ref[m, :, pl.ds(2 * HD, HD)] = low if which == 0 else high
                turned = jnp.transpose(part)
                for h in range(heads):
                    own = turned[h * FD : (h + 1) * FD]
                    turned_ref[m, h, pl.ds(0, FD), :] = own
                    turned_ref[m, h, pl.ds(FD, FD), :] = own

        for j in range(vchunks):
            halo_wait(1 + j)
            for m in range(windows):
                for c in range(CHUNK // HD):
                    at = j * CHUNK + c * HD
                    v_ref[m, :, pl.ds(at, HD)] = conv(
                        m, pl.ds(CHUNK + at, HD), cv_ref, pl.ds(at, HD)
                    ).astype(BF16)

        def state_copy(h):
            return pltpu.make_async_remote_copy(
                src_ref=fwd_ref.at[h],
                dst_ref=got_ref.at[h],
                send_sem=st_send.at[h],
                recv_sem=st_recv.at[h],
                device_id={"ctx": ctx + 1},
                device_id_type=MESH,
            )

        def head_lanes(h):
            return pl.ds(pl.multiple_of(h * HD, HD), HD)

        def inside(m):
            return jnp.logical_and(starts[m] >= first, starts[m] < first + span)

        def states(h, carry):
            for m in range(windows):
                kept = jnp.logical_or(lane_pos >= starts[m], jnp.logical_not(inside(m)))
                feats = jnp.where(kept, features(kt_ref, (m, h)), 0.0).astype(BF16)
                state = jnp.dot(feats, v_ref[m, :, head_lanes(h)], preferred_element_type=F32)
                bs_ref[h, m] = state

                @pl.when(ctx == 0)
                def _():
                    fwd_ref[h, m] = state.astype(BF16)

            @pl.when(jnp.logical_and(ctx == 0, ctx_n > 1))
            def _():
                state_copy(h).start()

            return carry

        lax.fori_loop(0, heads, states, 0)

        row_pos = lax.broadcasted_iota(jnp.int32, (span, span), 0)
        other_pos = lax.broadcasted_iota(jnp.int32, (span, span), 1)
        lane_head = (lax.broadcasted_iota(jnp.int32, (1, 3 * HD), 1) % HD) // FD
        lag = hop_lag * jnp.maximum(ctx - 1, 0)

        def step(i, carry):
            late = i - lag
            due = jnp.logical_and(late >= 0, late < heads)

            @pl.when(jnp.logical_and(due, ctx > 0))
            def _():
                state_copy(late).wait_recv()

                @pl.when(ctx < ctx_n - 1)
                def _():
                    for m in range(windows):
                        old = got_ref[late, m].astype(F32)
                        fwd_ref[late, m] = (bs_ref[late, m] + jnp.where(inside(m), 0.0, old)).astype(BF16)
                    state_copy(late).start()

            @pl.when(i < heads)
            def _():
                for m in range(windows):
                    mine = jnp.where(lane_head == i, q3_ref[m], jnp.zeros((), BF16))
                    s = lax.dot_general(
                        mine, k3_ref[m], (((1,), (1,)), ((), ())), preferred_element_type=F32
                    ) * (1.0 / math.sqrt(FD))
                    edge = starts[m] - first
                    allowed = jnp.logical_and(
                        other_pos <= row_pos, (other_pos >= edge) == (row_pos >= edge)
                    )
                    weight = jnp.where(allowed, 1.0 + s + 0.5 * s * s, 0.0).astype(BF16)
                    num_ref[m, :, head_lanes(i)] = jnp.dot(
                        weight, v_ref[m, :, head_lanes(i)], preferred_element_type=F32
                    )

            @pl.when(due)
            def _():
                @pl.when(ctx > 0)
                def _():
                    for m in range(windows):
                        feats = features(qt_ref, (m, late)).astype(BF16)
                        far = lax.dot_general(
                            feats, got_ref[late, m], (((0,), (0,)), ((), ())), preferred_element_type=F32
                        )
                        used = jnp.logical_or(col_pos < starts[m], starts[m] < first)
                        num_ref[m, :, head_lanes(late)] += jnp.where(used, far, 0.0)

                for m in range(windows):
                    num = num_ref[m, :, head_lanes(late)]
                    square = jnp.mean(num * num, axis=1, keepdims=True)
                    gain = vg_ref[:, head_lanes(late)].astype(F32)
                    mix_ref[pl.ds(m * span, span), head_lanes(late)] = (num * lax.rsqrt(square + EPS) * gain).astype(BF16)

            return carry

        lax.fori_loop(0, steps, step, 0)

        def part_copy(j):
            return pltpu.make_async_remote_copy(
                src_ref=part_ref.at[j],
                dst_ref=other_ref.at[j],
                send_sem=p_send.at[j],
                recv_sem=p_recv.at[j],
                device_id={"head": mate},
                device_id_type=MESH,
            )

        wo_load.wait()
        for j in range(vchunks):
            at = pl.ds(pl.multiple_of(mate * half + j * CHUNK, CHUNK), CHUNK)
            part_ref[j] = jnp.dot(mix_ref[...], wo_v[:, at], preferred_element_type=F32)
            part_copy(j).start()

        window_rows = span * ctx_n
        valid = jnp.concatenate(
            [
                jnp.where(
                    first + lax.broadcasted_iota(jnp.int32, (span, CHUNK), 0) < window_rows - pad_ref[m], 1.0, 0.0
                )
                for m in range(windows)
            ],
            axis=0,
        )
        for j in range(vchunks):
            at = pl.ds(pl.multiple_of(core * half + j * CHUNK, CHUNK), CHUNK)
            mine = jnp.dot(mix_ref[...], wo_v[:, at], preferred_element_type=F32)
            part_copy(j).wait_recv()
            update = (mine + other_ref[j]) * valid
            out_ref[:, cols(j)] = (x_ref[core, :, cols(j)].astype(F32) + update).astype(BF16)

            @pl.when(sec < sec_n - 1)
            def _():
                section_copy(j).start()

        for j in range(vchunks):
            mate_copy(j).wait_send()
            part_copy(j).wait_send()

            @pl.when(sec < sec_n - 1)
            def _():
                section_copy(j).wait_send()

        @pl.when(ctx < ctx_n - 1)
        def _():
            for j in range(vchunks + 1):
                halo_copy(j).wait_send()

            def sent(h, carry):
                state_copy(h).wait_send()
                return carry

            lax.fori_loop(0, heads, sent, 0)

    return kernel


def local(
    tokens, norm_gain, w_query, w_key, w_value, conv_query, conv_key, conv_value, value_gain, w_out, doc_start, pad_length
):
    windows, span, half = tokens.shape
    width = 2 * half
    rows_n = windows * span
    heads = half // HD
    vchunks = half // CHUNK
    sizes = (lax.axis_size("ctx"), lax.axis_size("section"), windows, span, width, conv_query.shape[1])
    vmem = pl.BlockSpec(memory_space=pltpu.VMEM)
    smem = pl.BlockSpec(memory_space=pltpu.SMEM)
    hbm = pl.BlockSpec(memory_space=pl.ANY)
    dma = pltpu.SemaphoreType.DMA
    out = pl.pallas_call(
        make_kernel(sizes),
        out_shape=jax.ShapeDtypeStruct((rows_n, half), BF16),
        in_specs=[smem, smem, vmem, vmem, hbm, hbm, hbm, vmem, vmem, vmem, vmem, hbm],
        out_specs=vmem,
        scratch_shapes=[
            pltpu.VMEM((width, half + CHUNK), BF16),
            pltpu.VMEM((half, width), BF16),
            pltpu.VMEM((2, rows_n, half), BF16),
            pltpu.VMEM((rows_n, width), BF16),
            pltpu.VMEM((windows, span + 8, half + CHUNK), F32),
            pltpu.VMEM((windows, span, 3 * HD), BF16),
            pltpu.VMEM((windows, span, 3 * HD), BF16),
            pltpu.VMEM((windows, heads, 2 * FD, span), F32),
            pltpu.VMEM((windows, heads, 2 * FD, span), F32),
            pltpu.VMEM((windows, span, half), BF16),
            pltpu.VMEM((heads, windows, FROWS, HD), F32),
            pltpu.VMEM((heads, windows, FROWS, HD), BF16),
            pltpu.VMEM((heads, windows, FROWS, HD), BF16),
            pltpu.VMEM((windows, span, half), F32),
            pltpu.VMEM((rows_n, half), BF16),
            pltpu.VMEM((vchunks, rows_n, CHUNK), F32),
            pltpu.VMEM((vchunks, rows_n, CHUNK), F32),
            dma((3 + vchunks,)),
            dma((vchunks,)),
            dma((vchunks,)),
            dma((vchunks,)),
            dma((vchunks,)),
            dma((vchunks + 1,)),
            dma((vchunks + 1,)),
            dma((heads,)),
            dma((heads,)),
            dma((vchunks,)),
            dma((vchunks,)),
        ],
        compiler_params=pltpu.CompilerParams(
            collective_id=0, has_side_effects=True, vmem_limit_bytes=48 * 1024 * 1024
        ),
        name="layers",
    )(
        doc_start, pad_length, tokens.reshape(rows_n, half), norm_gain, w_query, w_key, w_value,
        conv_query, conv_key, conv_value, value_gain, w_out,
    )
    return out.reshape(1, windows, span, half)


def solution(mesh):
    return jax.shard_map(
        local,
        mesh=mesh,
        in_specs=(
            P("groups", "ctx", "head"),
            P("section", None),
            P("section", None, "head"),
            P("section", None, "head"),
            P("section", None, "head"),
            P("section", None, "head"),
            P("section", None, "head"),
            P("section", None, "head"),
            P("section", "head"),
            P("section", "head", None),
            P("groups"),
            P("groups"),
        ),
        out_specs=P("section", "groups", "ctx", "head"),
        check_vma=False,
    )
```

```python
import math

import jax
import jax.numpy as jnp
from jax import lax
from jax.experimental import pallas as pl
from jax.experimental.pallas import tpu as pltpu
from jax.sharding import PartitionSpec as P

HD = 128
FD = 16
FROWS = 160
CHUNK = 256
EPS = 1e-06
MESH = pl.DeviceIdType.MESH
F32 = jnp.float32
BF16 = jnp.bfloat16


def features(doubled, first):
    x = doubled[first + (pl.ds(0, FD), slice(None))]
    rows = [x * (1.0 / FD**0.25), x * x * (1.0 / math.sqrt(2.0 * FD))]
    for d in range(1, FD // 2):
        rows.append(x * doubled[first + (pl.ds(d, FD), slice(None))] * (1.0 / math.sqrt(FD)))
    half = FD // 2
    rows.append(x[:half] * x[half:] * (1.0 / math.sqrt(FD)))
    lead = lax.broadcasted_iota(jnp.int32, (half, x.shape[1]), 0) == 0
    rows.append(jnp.where(lead, 1.0, 0.0))
    return jnp.concatenate(rows, axis=0)


def make_kernel(sizes):
    ctx_n, sec_n, windows, span, width, taps = sizes
    half = width // 2
    rows_n = windows * span
    heads = half // HD
    vchunks = half // CHUNK
    pair = heads // vchunks

    def kernel(
        start_in, pad_in, tok_in, gain_in, wq_ref, wk_ref, wv_ref, cq_in, ck_in, cv_in, vg_in, wo_ref,
        out_ref,
        start_ref, pad_ref, gain_ref, cq_ref, ck_ref, cv_ref, vg_ref, small_sem,
        w_all, wo_v, x_ref, n_ref, pr_ref, q3_ref, k3_ref, qt_ref, kt_ref, v_ref, bs_ref, got_ref, fwd_ref,
        num_ref, mix_ref, part_ref, other_ref,
        w_sem, x_send, x_recv, sec_send, sec_recv, halo_send, halo_recv, st_send, st_recv, p_send, p_recv,
    ):
        ctx = lax.axis_index("ctx")
        sec = lax.axis_index("section")
        core = lax.axis_index("head")
        mate = 1 - core

        tok_load = pltpu.make_async_copy(tok_in, x_ref.at[core], small_sem.at[0])

        @pl.when(sec == 0)
        def _():
            tok_load.start()

        small = [
            pltpu.make_async_copy(source, target, small_sem.at[1 + i])
            for i, (source, target) in enumerate(
                (
                    (gain_in, gain_ref),
                    (start_in, start_ref),
                    (pad_in, pad_ref),
                    (cq_in, cq_ref),
                    (ck_in, ck_ref),
                    (cv_in, cv_ref),
                    (vg_in, vg_ref),
                )
            )
        ]
        for load in small:
            load.start()

        loads = [
            pltpu.make_async_copy(wq_ref.at[0], w_all.at[:, pl.ds(0, HD)], w_sem.at[0]),
            pltpu.make_async_copy(wk_ref.at[0], w_all.at[:, pl.ds(HD, HD)], w_sem.at[1]),
        ]
        for j in range(vchunks):
            loads.append(
                pltpu.make_async_copy(
                    wv_ref.at[0, :, pl.ds(j * CHUNK, CHUNK)],
                    w_all.at[:, pl.ds((j + 1) * CHUNK, CHUNK)],
                    w_sem.at[2 + j],
                )
            )
        wo_load = pltpu.make_async_copy(wo_ref.at[0], wo_v, w_sem.at[2 + vchunks])
        for load in loads:
            load.start()
        wo_load.start()

        barrier = pltpu.get_barrier_semaphore()
        pl.semaphore_signal(barrier, inc=1, device_id={"head": mate}, device_id_type=MESH)

        @pl.when(ctx > 0)
        def _():
            pl.semaphore_signal(barrier, inc=1, device_id={"ctx": ctx - 1}, device_id_type=MESH)

        @pl.when(ctx < ctx_n - 1)
        def _():
            pl.semaphore_signal(barrier, inc=1, device_id={"ctx": ctx + 1}, device_id_type=MESH)

        @pl.when(sec > 0)
        def _():
            pl.semaphore_signal(barrier, inc=1, device_id={"section": sec - 1}, device_id_type=MESH)

        @pl.when(sec < sec_n - 1)
        def _():
            pl.semaphore_signal(barrier, inc=1, device_id={"section": sec + 1}, device_id_type=MESH)

        peers = (
            1
            + jnp.where(ctx > 0, 1, 0)
            + jnp.where(ctx < ctx_n - 1, 1, 0)
            + jnp.where(sec > 0, 1, 0)
            + jnp.where(sec < sec_n - 1, 1, 0)
        )
        pl.semaphore_wait(barrier, peers)

        def cols(j):
            return pl.ds(j * CHUNK, CHUNK)

        def section_copy(j):
            return pltpu.make_async_remote_copy(
                src_ref=out_ref.at[:, cols(j)],
                dst_ref=x_ref.at[core, :, cols(j)],
                send_sem=sec_send.at[j],
                recv_sem=sec_recv.at[j],
                device_id={"section": sec + 1},
                device_id_type=MESH,
            )

        def mate_copy(j):
            return pltpu.make_async_remote_copy(
                src_ref=x_ref.at[core, :, cols(j)],
                dst_ref=x_ref.at[core, :, cols(j)],
                send_sem=x_send.at[j],
                recv_sem=x_recv.at[j],
                device_id={"head": mate},
                device_id_type=MESH,
            )

        @pl.when(sec == 0)
        def _():
            tok_load.wait()

        for j in range(vchunks):

            @pl.when(sec > 0)
            def _():
                section_copy(j).wait_recv()

            mate_copy(j).start()

        for load in small:
            load.wait()

        first = ctx * span
        col_pos = first + lax.broadcasted_iota(jnp.int32, (span, HD), 0)
        lane_pos = first + lax.broadcasted_iota(jnp.int32, (1, span), 1)
        starts = [start_ref[m] for m in range(windows)]

        for j in range(vchunks):
            mate_copy(j).wait_recv()

        block = 32

        def norm_rows(i, carry):
            at = pl.ds(pl.multiple_of(i * block, block), block)
            left = x_ref[0, at, :].astype(F32)
            right = x_ref[1, at, :].astype(F32)
            square = jnp.sum(left * left, axis=1, keepdims=True) + jnp.sum(right * right, axis=1, keepdims=True)
            scale = lax.rsqrt(square * (1.0 / width) + EPS)
            n_ref[at, pl.ds(0, half)] = (left * scale * gain_ref[:, pl.ds(0, half)].astype(F32)).astype(BF16)
            n_ref[at, pl.ds(half, half)] = (right * scale * gain_ref[:, pl.ds(half, half)].astype(F32)).astype(BF16)
            return carry

        lax.fori_loop(0, rows_n // block, norm_rows, 0)

        def halo_copy(j):
            return pltpu.make_async_remote_copy(
                src_ref=pr_ref.at[:, pl.ds(span, 8), cols(j)],
                dst_ref=pr_ref.at[:, pl.ds(0, 8), cols(j)],
                send_sem=halo_send.at[j],
                recv_sem=halo_recv.at[j],
                device_id={"ctx": ctx + 1},
                device_id_type=MESH,
            )

        @pl.when(ctx == 0)
        def _():
            pr_ref[:, pl.ds(0, 8), :] = jnp.zeros((windows, 8, half + CHUNK), F32)

        def conv(m, at, taps_ref, tap_at):
            after = col_pos >= starts[m]
            total = None
            for j in range(taps):
                source = pr_ref[m, pl.ds(8 - j, span), at]
                term = taps_ref[0, pl.ds(j, 1), tap_at].astype(F32) * source
                if j:
                    same = (col_pos - j >= starts[m]) == after
                    term = jnp.where(same, term, 0.0)
                total = term if total is None else total + term
            return total

        def halo_wait(j):
            @pl.when(ctx > 0)
            def _():
                halo_copy(j).wait_recv()

        def project(j):
            if j == 0:
                loads[0].wait()
                loads[1].wait()
            else:
                loads[1 + j].wait()
            got = jnp.dot(n_ref[...], w_all[:, cols(j)], preferred_element_type=F32).astype(BF16).astype(F32)
            for m in range(windows):
                pr_ref[m, pl.ds(8, span), cols(j)] = got[m * span : (m + 1) * span]

            @pl.when(ctx < ctx_n - 1)
            def _():
                halo_copy(j).start()

        def conv_query_key():
            halo_wait(0)
            for m in range(windows):
                for which, taps_ref, wide_ref, turned_ref in ((1, ck_ref, k3_ref, kt_ref), (0, cq_ref, q3_ref, qt_ref)):
                    part = conv(m, pl.ds(which * HD, HD), taps_ref, pl.ds(0, HD))
                    high = part.astype(BF16)
                    low = (part - high.astype(F32)).astype(BF16)
                    wide_ref[m, :, pl.ds(0, HD)] = high
                    wide_ref[m, :, pl.ds(HD, HD)] = high if which == 0 else low
                    wide_ref[m, :, pl.ds(2 * HD, HD)] = low if which == 0 else high
                    turned = jnp.transpose(part)
                    for h in range(heads):
                        own = turned[h * FD : (h + 1) * FD]
                        turned_ref[m, h, pl.ds(0, FD), :] = own
                        turned_ref[m, h, pl.ds(FD, FD), :] = own

        def conv_values(j):
            halo_wait(1 + j)
            for m in range(windows):
                for c in range(CHUNK // HD):
                    at = j * CHUNK + c * HD
                    v_ref[m, :, pl.ds(at, HD)] = conv(m, pl.ds(CHUNK + at, HD), cv_ref, pl.ds(at, HD)).astype(BF16)

        def state_copy(h):
            return pltpu.make_async_remote_copy(
                src_ref=fwd_ref.at[h],
                dst_ref=got_ref.at[h],
                send_sem=st_send.at[h],
                recv_sem=st_recv.at[h],
                device_id={"ctx": ctx + 1},
                device_id_type=MESH,
            )

        def head_lanes(h):
            return pl.ds(pl.multiple_of(h * HD, HD), HD)

        def inside(m):
            return jnp.logical_and(starts[m] >= first, starts[m] < first + span)

        def states(p):
            for h in range(p * pair, (p + 1) * pair):
                made = []
                for m in range(windows):
                    kept = jnp.logical_or(lane_pos >= starts[m], jnp.logical_not(inside(m)))
                    feats = jnp.where(kept, features(kt_ref, (m, h)), 0.0).astype(BF16)
                    made.append(jnp.dot(feats, v_ref[m, :, pl.ds(h * HD, HD)], preferred_element_type=F32))

                @pl.when(ctx == 0)
                def _():
                    for m in range(windows):
                        fwd_ref[h, m] = made[m].astype(BF16)
                    if ctx_n > 1:
                        state_copy(h).start()

                @pl.when(ctx > 0)
                def _():
                    for m in range(windows):
                        bs_ref[h, m] = made[m]

        def pass_on(t):
            p = t - 2 - ctx
            due = jnp.logical_and(p >= 0, p < vchunks)
            middle = jnp.logical_and(ctx > 0, ctx < ctx_n - 1)

            @pl.when(jnp.logical_and(due, middle))
            def _():
                def one(i, carry):
                    h = p * pair + i
                    state_copy(h).wait_recv()
                    for m in range(windows):
                        old = got_ref[h, m].astype(F32)
                        fwd_ref[h, m] = (bs_ref[h, m] + jnp.where(inside(m), 0.0, old)).astype(BF16)
                    state_copy(h).start()
                    return carry

                lax.fori_loop(0, pair, one, 0)

        project(0)
        for t in range(1, vchunks + 2):
            if t <= vchunks:
                project(t)
            if t == 1:
                conv_query_key()
            else:
                conv_values(t - 2)
                states(t - 2)
            if t >= 3:
                pass_on(t)

        row_pos = lax.broadcasted_iota(jnp.int32, (span, span), 0)
        other_pos = lax.broadcasted_iota(jnp.int32, (span, span), 1)
        lane_head = (lax.broadcasted_iota(jnp.int32, (1, 3 * HD), 1) % HD) // FD
        local_steps = max(vchunks, ctx_n - 2)

        def local_part(lp, carry):
            pass_on(vchunks + 2 + lp)

            @pl.when(lp < vchunks)
            def _():
                for c in range(pair):
                    h = lp * pair + c
                    for m in range(windows):
                        mine = jnp.where(lane_head == h, q3_ref[m], jnp.zeros((), BF16))
                        s = lax.dot_general(
                            mine, k3_ref[m], (((1,), (1,)), ((), ())), preferred_element_type=F32
                        ) * (1.0 / math.sqrt(FD))
                        edge = starts[m] - first
                        allowed = jnp.logical_and(other_pos <= row_pos, (other_pos >= edge) == (row_pos >= edge))
                        weight = jnp.where(allowed, 1.0 + s + 0.5 * s * s, 0.0).astype(BF16)
                        num_ref[m, :, head_lanes(h)] = jnp.dot(
                            weight, v_ref[m, :, head_lanes(h)], preferred_element_type=F32
                        )

            return carry

        lax.fori_loop(0, local_steps, local_part, 0)

        def finish(h, carry):
            @pl.when(ctx > 0)
            def _():
                @pl.when(ctx == ctx_n - 1)
                def _():
                    state_copy(h).wait_recv()

                for m in range(windows):
                    feats = features(qt_ref, (m, h)).astype(BF16)
                    far = lax.dot_general(
                        feats, got_ref[h, m], (((0,), (0,)), ((), ())), preferred_element_type=F32
                    )
                    used = jnp.logical_or(col_pos < starts[m], starts[m] < first)
                    num_ref[m, :, head_lanes(h)] += jnp.where(used, far, 0.0)

            for m in range(windows):
                num = num_ref[m, :, head_lanes(h)]
                square = jnp.mean(num * num, axis=1, keepdims=True)
                gain = vg_ref[:, head_lanes(h)].astype(F32)
                mix_ref[pl.ds(m * span, span), head_lanes(h)] = (num * lax.rsqrt(square + EPS) * gain).astype(BF16)
            return carry

        lax.fori_loop(0, heads, finish, 0)

        def part_copy(j):
            return pltpu.make_async_remote_copy(
                src_ref=part_ref.at[j],
                dst_ref=other_ref.at[j],
                send_sem=p_send.at[j],
                recv_sem=p_recv.at[j],
                device_id={"head": mate},
                device_id_type=MESH,
            )

        wo_load.wait()
        for j in range(vchunks):
            at = pl.ds(pl.multiple_of(mate * half + j * CHUNK, CHUNK), CHUNK)
            part_ref[j] = jnp.dot(mix_ref[...], wo_v[:, at], preferred_element_type=F32)
            part_copy(j).start()

        window_rows = span * ctx_n
        valid = jnp.concatenate(
            [
                jnp.where(
                    first + lax.broadcasted_iota(jnp.int32, (span, CHUNK), 0) < window_rows - pad_ref[m], 1.0, 0.0
                )
                for m in range(windows)
            ],
            axis=0,
        )
        for j in range(vchunks):
            at = pl.ds(pl.multiple_of(core * half + j * CHUNK, CHUNK), CHUNK)
            mine = jnp.dot(mix_ref[...], wo_v[:, at], preferred_element_type=F32)
            part_copy(j).wait_recv()
            update = (mine + other_ref[j]) * valid
            out_ref[:, cols(j)] = (x_ref[core, :, cols(j)].astype(F32) + update).astype(BF16)

            @pl.when(sec < sec_n - 1)
            def _():
                section_copy(j).start()

        for j in range(vchunks):
            mate_copy(j).wait_send()
            part_copy(j).wait_send()

            @pl.when(sec < sec_n - 1)
            def _():
                section_copy(j).wait_send()

        @pl.when(ctx < ctx_n - 1)
        def _():
            for j in range(vchunks + 1):
                halo_copy(j).wait_send()

            def sent(h, carry):
                state_copy(h).wait_send()
                return carry

            lax.fori_loop(0, heads, sent, 0)

    return kernel


def local(
    tokens, norm_gain, w_query, w_key, w_value, conv_query, conv_key, conv_value, value_gain, w_out, doc_start, pad_length
):
    windows, span, half = tokens.shape
    width = 2 * half
    rows_n = windows * span
    heads = half // HD
    vchunks = half // CHUNK
    sizes = (lax.axis_size("ctx"), lax.axis_size("section"), windows, span, width, conv_query.shape[1])
    vmem = pl.BlockSpec(memory_space=pltpu.VMEM)
    hbm = pl.BlockSpec(memory_space=pltpu.MemorySpace.HBM)
    dma = pltpu.SemaphoreType.DMA
    out = pl.pallas_call(
        make_kernel(sizes),
        out_shape=jax.ShapeDtypeStruct((rows_n, half), BF16),
        in_specs=[hbm] * 12,
        out_specs=vmem,
        scratch_shapes=[
            pltpu.SMEM((windows,), jnp.int32),
            pltpu.SMEM((windows,), jnp.int32),
            pltpu.VMEM(norm_gain.shape, BF16),
            pltpu.VMEM(conv_query.shape, BF16),
            pltpu.VMEM(conv_key.shape, BF16),
            pltpu.VMEM(conv_value.shape, BF16),
            pltpu.VMEM(value_gain.shape, BF16),
            dma((8,)),
            pltpu.VMEM((width, half + CHUNK), BF16),
            pltpu.VMEM((half, width), BF16),
            pltpu.VMEM((2, rows_n, half), BF16),
            pltpu.VMEM((rows_n, width), BF16),
            pltpu.VMEM((windows, span + 8, half + CHUNK), F32),
            pltpu.VMEM((windows, span, 3 * HD), BF16),
            pltpu.VMEM((windows, span, 3 * HD), BF16),
            pltpu.VMEM((windows, heads, 2 * FD, span), F32),
            pltpu.VMEM((windows, heads, 2 * FD, span), F32),
            pltpu.VMEM((windows, span, half), BF16),
            pltpu.VMEM((heads, windows, FROWS, HD), F32),
            pltpu.VMEM((heads, windows, FROWS, HD), BF16),
            pltpu.VMEM((heads, windows, FROWS, HD), BF16),
            pltpu.VMEM((windows, span, half), F32),
            pltpu.VMEM((rows_n, half), BF16),
            pltpu.VMEM((vchunks, rows_n, CHUNK), F32),
            pltpu.VMEM((vchunks, rows_n, CHUNK), F32),
            dma((3 + vchunks,)),
            dma((vchunks,)),
            dma((vchunks,)),
            dma((vchunks,)),
            dma((vchunks,)),
            dma((vchunks + 1,)),
            dma((vchunks + 1,)),
            dma((heads,)),
            dma((heads,)),
            dma((vchunks,)),
            dma((vchunks,)),
        ],
        compiler_params=pltpu.CompilerParams(
            collective_id=0, has_side_effects=True, vmem_limit_bytes=60 * 1024 * 1024
        ),
        name="layers",
    )(
        doc_start, pad_length, tokens.reshape(rows_n, half), norm_gain, w_query, w_key, w_value,
        conv_query, conv_key, conv_value, value_gain, w_out,
    )
    return out.reshape(1, windows, span, half)


def solution(mesh):
    return jax.shard_map(
        local,
        mesh=mesh,
        in_specs=(
            P("groups", "ctx", "head"),
            P("section", None),
            P("section", None, "head"),
            P("section", None, "head"),
            P("section", None, "head"),
            P("section", None, "head"),
            P("section", None, "head"),
            P("section", None, "head"),
            P("section", "head"),
            P("section", "head", None),
            P("groups"),
            P("groups"),
        ),
        out_specs=P("section", "groups", "ctx", "head"),
        check_vma=False,
    )
```

```python
import math

import jax
import jax.numpy as jnp
from jax import lax
from jax.experimental import pallas as pl
from jax.experimental.pallas import tpu as pltpu
from jax.sharding import PartitionSpec as P

HD = 128
FD = 16
FROWS = 160
CHUNK = 256
EPS = 1e-06
MESH = pl.DeviceIdType.MESH
F32 = jnp.float32
BF16 = jnp.bfloat16


def features(doubled, first):
    x = doubled[first + (pl.ds(0, FD), slice(None))]
    rows = [x * (1.0 / FD**0.25), x * x * (1.0 / math.sqrt(2.0 * FD))]
    for d in range(1, FD // 2):
        rows.append(x * doubled[first + (pl.ds(d, FD), slice(None))] * (1.0 / math.sqrt(FD)))
    half = FD // 2
    rows.append(x[:half] * x[half:] * (1.0 / math.sqrt(FD)))
    lead = lax.broadcasted_iota(jnp.int32, (half, x.shape[1]), 0) == 0
    rows.append(jnp.where(lead, 1.0, 0.0))
    return jnp.concatenate(rows, axis=0)


def make_kernel(sizes):
    ctx_n, sec_n, windows, span, width, taps = sizes
    half = width // 2
    rows_n = windows * span
    heads = half // HD
    vchunks = half // CHUNK
    pair = heads // vchunks
    relay = sec_n % 2 == 0 and ctx_n > 1 and pair % 2 == 0

    def kernel(
        start_in, pad_in, tok_in, gain_in, wq_ref, wk_ref, wv_ref, cq_in, ck_in, cv_in, vg_in, wo_ref,
        out_ref,
        start_ref, pad_ref, gain_ref, cq_ref, ck_ref, cv_ref, vg_ref, small_sem,
        w_all, wo_v, x_ref, n_ref, pr_ref, q3_ref, k3_ref, qt_ref, kt_ref, v_ref, bs_ref, got_ref, fwd_ref,
        num_ref, mix_ref, part_ref, other_ref, rel_ref, rel_send, rel_recv,
        w_sem, x_send, x_recv, sec_send, sec_recv, halo_send, halo_recv, st_send, st_recv, p_send, p_recv,
    ):
        ctx = lax.axis_index("ctx")
        sec = lax.axis_index("section")
        core = lax.axis_index("head")
        mate = 1 - core

        tok_load = pltpu.make_async_copy(tok_in, x_ref.at[core], small_sem.at[0])

        @pl.when(sec == 0)
        def _():
            tok_load.start()

        small = [
            pltpu.make_async_copy(source, target, small_sem.at[1 + i])
            for i, (source, target) in enumerate(
                (
                    (gain_in, gain_ref),
                    (start_in, start_ref),
                    (pad_in, pad_ref),
                    (cq_in, cq_ref),
                    (ck_in, ck_ref),
                    (cv_in, cv_ref),
                    (vg_in, vg_ref),
                )
            )
        ]
        for load in small:
            load.start()

        loads = [
            pltpu.make_async_copy(wq_ref.at[0], w_all.at[:, pl.ds(0, HD)], w_sem.at[0]),
            pltpu.make_async_copy(wk_ref.at[0], w_all.at[:, pl.ds(HD, HD)], w_sem.at[1]),
        ]
        for j in range(vchunks):
            loads.append(
                pltpu.make_async_copy(
                    wv_ref.at[0, :, pl.ds(j * CHUNK, CHUNK)],
                    w_all.at[:, pl.ds((j + 1) * CHUNK, CHUNK)],
                    w_sem.at[2 + j],
                )
            )
        wo_load = pltpu.make_async_copy(wo_ref.at[0], wo_v, w_sem.at[2 + vchunks])
        for load in loads:
            load.start()
        wo_load.start()

        barrier = pltpu.get_barrier_semaphore()
        pl.semaphore_signal(barrier, inc=1, device_id={"head": mate}, device_id_type=MESH)

        @pl.when(ctx > 0)
        def _():
            pl.semaphore_signal(barrier, inc=1, device_id={"ctx": ctx - 1}, device_id_type=MESH)

        @pl.when(ctx < ctx_n - 1)
        def _():
            pl.semaphore_signal(barrier, inc=1, device_id={"ctx": ctx + 1}, device_id_type=MESH)

        @pl.when(sec > 0)
        def _():
            pl.semaphore_signal(barrier, inc=1, device_id={"section": sec - 1}, device_id_type=MESH)

        @pl.when(sec < sec_n - 1)
        def _():
            pl.semaphore_signal(barrier, inc=1, device_id={"section": sec + 1}, device_id_type=MESH)

        peers = (
            1
            + jnp.where(ctx > 0, 1, 0)
            + jnp.where(ctx < ctx_n - 1, 1, 0)
            + jnp.where(sec > 0, 1, 0)
            + jnp.where(sec < sec_n - 1, 1, 0)
        )
        across = sec + 1 - 2 * (sec % 2)
        if relay:

            @pl.when(ctx > 0)
            def _():
                pl.semaphore_signal(
                    barrier, inc=1, device_id={"ctx": ctx - 1, "section": across}, device_id_type=MESH
                )

            @pl.when(ctx < ctx_n - 1)
            def _():
                pl.semaphore_signal(
                    barrier, inc=1, device_id={"ctx": ctx + 1, "section": across}, device_id_type=MESH
                )

            peers = peers + jnp.where(ctx > 0, 1, 0) + jnp.where(ctx < ctx_n - 1, 1, 0)
        pl.semaphore_wait(barrier, peers)

        def relay_copy(r):
            return pltpu.make_async_remote_copy(
                src_ref=rel_ref.at[r],
                dst_ref=got_ref.at[2 * r],
                send_sem=rel_send.at[r],
                recv_sem=st_recv.at[2 * r],
                device_id={"section": across},
                device_id_type=MESH,
            )

        def detour_copy(r):
            return pltpu.make_async_remote_copy(
                src_ref=fwd_ref.at[2 * r],
                dst_ref=rel_ref.at[r],
                send_sem=st_send.at[2 * r],
                recv_sem=rel_recv.at[r],
                device_id={"ctx": ctx + 1, "section": across},
                device_id_type=MESH,
            )

        def relay_all(parity):
            if relay:

                @pl.when(jnp.logical_and(sec % 2 == parity, ctx > 0))
                def _():
                    def one(r, carry):
                        detour_copy(r).wait_recv()
                        relay_copy(r).start()
                        return carry

                    lax.fori_loop(0, heads // 2, one, 0)

        relay_all(1)

        def cols(j):
            return pl.ds(j * CHUNK, CHUNK)

        def section_copy(j):
            return pltpu.make_async_remote_copy(
                src_ref=out_ref.at[:, cols(j)],
                dst_ref=x_ref.at[core, :, cols(j)],
                send_sem=sec_send.at[j],
                recv_sem=sec_recv.at[j],
                device_id={"section": sec + 1},
                device_id_type=MESH,
            )

        def mate_copy(j):
            return pltpu.make_async_remote_copy(
                src_ref=x_ref.at[core, :, cols(j)],
                dst_ref=x_ref.at[core, :, cols(j)],
                send_sem=x_send.at[j],
                recv_sem=x_recv.at[j],
                device_id={"head": mate},
                device_id_type=MESH,
            )

        @pl.when(sec == 0)
        def _():
            tok_load.wait()

        for j in range(vchunks):

            @pl.when(sec > 0)
            def _():
                section_copy(j).wait_recv()

            mate_copy(j).start()

        for load in small:
            load.wait()

        first = ctx * span
        col_pos = first + lax.broadcasted_iota(jnp.int32, (span, HD), 0)
        lane_pos = first + lax.broadcasted_iota(jnp.int32, (1, span), 1)
        starts = [start_ref[m] for m in range(windows)]

        for j in range(vchunks):
            mate_copy(j).wait_recv()

        block = 32

        def norm_rows(i, carry):
            at = pl.ds(pl.multiple_of(i * block, block), block)
            left = x_ref[0, at, :].astype(F32)
            right = x_ref[1, at, :].astype(F32)
            square = jnp.sum(left * left, axis=1, keepdims=True) + jnp.sum(right * right, axis=1, keepdims=True)
            scale = lax.rsqrt(square * (1.0 / width) + EPS)
            n_ref[at, pl.ds(0, half)] = (left * scale * gain_ref[:, pl.ds(0, half)].astype(F32)).astype(BF16)
            n_ref[at, pl.ds(half, half)] = (right * scale * gain_ref[:, pl.ds(half, half)].astype(F32)).astype(BF16)
            return carry

        lax.fori_loop(0, rows_n // block, norm_rows, 0)

        def halo_copy(j):
            return pltpu.make_async_remote_copy(
                src_ref=pr_ref.at[:, pl.ds(span, 8), cols(j)],
                dst_ref=pr_ref.at[:, pl.ds(0, 8), cols(j)],
                send_sem=halo_send.at[j],
                recv_sem=halo_recv.at[j],
                device_id={"ctx": ctx + 1},
                device_id_type=MESH,
            )

        @pl.when(ctx == 0)
        def _():
            pr_ref[:, pl.ds(0, 8), :] = jnp.zeros((windows, 8, half + CHUNK), F32)

        def conv(m, at, taps_ref, tap_at):
            after = col_pos >= starts[m]
            total = None
            for j in range(taps):
                source = pr_ref[m, pl.ds(8 - j, span), at]
                term = taps_ref[0, pl.ds(j, 1), tap_at].astype(F32) * source
                if j:
                    same = (col_pos - j >= starts[m]) == after
                    term = jnp.where(same, term, 0.0)
                total = term if total is None else total + term
            return total

        def halo_wait(j):
            @pl.when(ctx > 0)
            def _():
                halo_copy(j).wait_recv()

        def project(j):
            if j == 0:
                loads[0].wait()
                loads[1].wait()
            else:
                loads[1 + j].wait()
            got = jnp.dot(n_ref[...], w_all[:, cols(j)], preferred_element_type=F32).astype(BF16).astype(F32)
            for m in range(windows):
                pr_ref[m, pl.ds(8, span), cols(j)] = got[m * span : (m + 1) * span]

            @pl.when(ctx < ctx_n - 1)
            def _():
                halo_copy(j).start()

        def conv_query_key():
            halo_wait(0)
            for m in range(windows):
                for which, taps_ref, wide_ref, turned_ref in ((1, ck_ref, k3_ref, kt_ref), (0, cq_ref, q3_ref, qt_ref)):
                    part = conv(m, pl.ds(which * HD, HD), taps_ref, pl.ds(0, HD))
                    high = part.astype(BF16)
                    low = (part - high.astype(F32)).astype(BF16)
                    wide_ref[m, :, pl.ds(0, HD)] = high
                    wide_ref[m, :, pl.ds(HD, HD)] = high if which == 0 else low
                    wide_ref[m, :, pl.ds(2 * HD, HD)] = low if which == 0 else high
                    turned = jnp.transpose(part)
                    for h in range(heads):
                        own = turned[h * FD : (h + 1) * FD]
                        turned_ref[m, h, pl.ds(0, FD), :] = own
                        turned_ref[m, h, pl.ds(FD, FD), :] = own

        def conv_values(j):
            halo_wait(1 + j)
            for m in range(windows):
                for c in range(CHUNK // HD):
                    at = j * CHUNK + c * HD
                    v_ref[m, :, pl.ds(at, HD)] = conv(m, pl.ds(CHUNK + at, HD), cv_ref, pl.ds(at, HD)).astype(BF16)

        def state_copy(h):
            return pltpu.make_async_remote_copy(
                src_ref=fwd_ref.at[h],
                dst_ref=got_ref.at[h],
                send_sem=st_send.at[h],
                recv_sem=st_recv.at[h],
                device_id={"ctx": ctx + 1},
                device_id_type=MESH,
            )

        def state_start(r, odd):
            if relay and odd == 0:
                detour_copy(r).start()
            else:
                state_copy(2 * r + odd).start()

        def head_lanes(h):
            return pl.ds(pl.multiple_of(h * HD, HD), HD)

        def inside(m):
            return jnp.logical_and(starts[m] >= first, starts[m] < first + span)

        def states(p):
            for h in range(p * pair, (p + 1) * pair):
                made = []
                for m in range(windows):
                    kept = jnp.logical_or(lane_pos >= starts[m], jnp.logical_not(inside(m)))
                    feats = jnp.where(kept, features(kt_ref, (m, h)), 0.0).astype(BF16)
                    made.append(jnp.dot(feats, v_ref[m, :, pl.ds(h * HD, HD)], preferred_element_type=F32))

                @pl.when(ctx == 0)
                def _():
                    for m in range(windows):
                        fwd_ref[h, m] = made[m].astype(BF16)
                    if ctx_n > 1:
                        state_start(h // 2, h % 2)

                @pl.when(ctx > 0)
                def _():
                    for m in range(windows):
                        bs_ref[h, m] = made[m]

        def pass_on(t):
            p = t - 2 - ctx
            due = jnp.logical_and(p >= 0, p < vchunks)
            middle = jnp.logical_and(ctx > 0, ctx < ctx_n - 1)

            @pl.when(jnp.logical_and(due, middle))
            def _():
                def one(i, carry):
                    h = p * pair + i
                    state_copy(h).wait_recv()
                    for m in range(windows):
                        old = got_ref[h, m].astype(F32)
                        fwd_ref[h, m] = (bs_ref[h, m] + jnp.where(inside(m), 0.0, old)).astype(BF16)
                    state_start(p * (pair // 2) + i // 2, i % 2)
                    return carry

                for i in range(pair):
                    one(i, 0)

        project(0)
        for t in range(1, vchunks + 2):
            if t <= vchunks:
                project(t)
            if t == 1:
                conv_query_key()
            else:
                conv_values(t - 2)
                states(t - 2)
            if t >= 3:
                pass_on(t)

        row_pos = lax.broadcasted_iota(jnp.int32, (span, span), 0)
        other_pos = lax.broadcasted_iota(jnp.int32, (span, span), 1)
        lane_head = (lax.broadcasted_iota(jnp.int32, (1, 3 * HD), 1) % HD) // FD
        local_steps = max(vchunks, ctx_n - 2)

        def local_part(lp, carry):
            pass_on(vchunks + 2 + lp)

            @pl.when(lp < vchunks)
            def _():
                for c in range(pair):
                    h = lp * pair + c
                    for m in range(windows):
                        mine = jnp.where(lane_head == h, q3_ref[m], jnp.zeros((), BF16))
                        s = lax.dot_general(
                            mine, k3_ref[m], (((1,), (1,)), ((), ())), preferred_element_type=F32
                        ) * (1.0 / math.sqrt(FD))
                        edge = starts[m] - first
                        allowed = jnp.logical_and(other_pos <= row_pos, (other_pos >= edge) == (row_pos >= edge))
                        weight = jnp.where(allowed, 1.0 + s + 0.5 * s * s, 0.0).astype(BF16)
                        num_ref[m, :, head_lanes(h)] = jnp.dot(
                            weight, v_ref[m, :, head_lanes(h)], preferred_element_type=F32
                        )

            return carry

        lax.fori_loop(0, local_steps, local_part, 0)

        def finish(h, carry):
            @pl.when(ctx > 0)
            def _():
                @pl.when(ctx == ctx_n - 1)
                def _():
                    state_copy(h).wait_recv()

                for m in range(windows):
                    feats = features(qt_ref, (m, h)).astype(BF16)
                    far = lax.dot_general(
                        feats, got_ref[h, m], (((0,), (0,)), ((), ())), preferred_element_type=F32
                    )
                    used = jnp.logical_or(col_pos < starts[m], starts[m] < first)
                    num_ref[m, :, head_lanes(h)] += jnp.where(used, far, 0.0)

            for m in range(windows):
                num = num_ref[m, :, head_lanes(h)]
                square = jnp.mean(num * num, axis=1, keepdims=True)
                gain = vg_ref[:, head_lanes(h)].astype(F32)
                mix_ref[pl.ds(m * span, span), head_lanes(h)] = (num * lax.rsqrt(square + EPS) * gain).astype(BF16)
            return carry

        lax.fori_loop(0, heads, finish, 0)

        def part_copy(j):
            return pltpu.make_async_remote_copy(
                src_ref=part_ref.at[j],
                dst_ref=other_ref.at[j],
                send_sem=p_send.at[j],
                recv_sem=p_recv.at[j],
                device_id={"head": mate},
                device_id_type=MESH,
            )

        wo_load.wait()
        for j in range(vchunks):
            at = pl.ds(pl.multiple_of(mate * half + j * CHUNK, CHUNK), CHUNK)
            part_ref[j] = jnp.dot(mix_ref[...], wo_v[:, at], preferred_element_type=F32)
            part_copy(j).start()

        window_rows = span * ctx_n
        valid = jnp.concatenate(
            [
                jnp.where(
                    first + lax.broadcasted_iota(jnp.int32, (span, CHUNK), 0) < window_rows - pad_ref[m], 1.0, 0.0
                )
                for m in range(windows)
            ],
            axis=0,
        )
        for j in range(vchunks):
            at = pl.ds(pl.multiple_of(core * half + j * CHUNK, CHUNK), CHUNK)
            mine = jnp.dot(mix_ref[...], wo_v[:, at], preferred_element_type=F32)
            part_copy(j).wait_recv()
            update = (mine + other_ref[j]) * valid
            out_ref[:, cols(j)] = (x_ref[core, :, cols(j)].astype(F32) + update).astype(BF16)

            @pl.when(sec < sec_n - 1)
            def _():
                section_copy(j).start()

        relay_all(0)

        if relay:

            @pl.when(ctx > 0)
            def _():
                def relayed(r, carry):
                    relay_copy(r).wait_send()
                    return carry

                lax.fori_loop(0, heads // 2, relayed, 0)

        for j in range(vchunks):
            mate_copy(j).wait_send()
            part_copy(j).wait_send()

            @pl.when(sec < sec_n - 1)
            def _():
                section_copy(j).wait_send()

        @pl.when(ctx < ctx_n - 1)
        def _():
            for j in range(vchunks + 1):
                halo_copy(j).wait_send()

            def sent(h, carry):
                state_copy(h).wait_send()
                return carry

            lax.fori_loop(0, heads, sent, 0)

    return kernel


def local(
    tokens, norm_gain, w_query, w_key, w_value, conv_query, conv_key, conv_value, value_gain, w_out, doc_start, pad_length
):
    windows, span, half = tokens.shape
    width = 2 * half
    rows_n = windows * span
    heads = half // HD
    vchunks = half // CHUNK
    sizes = (lax.axis_size("ctx"), lax.axis_size("section"), windows, span, width, conv_query.shape[1])
    vmem = pl.BlockSpec(memory_space=pltpu.VMEM)
    hbm = pl.BlockSpec(memory_space=pltpu.MemorySpace.HBM)
    dma = pltpu.SemaphoreType.DMA
    out = pl.pallas_call(
        make_kernel(sizes),
        out_shape=jax.ShapeDtypeStruct((rows_n, half), BF16),
        in_specs=[hbm] * 12,
        out_specs=vmem,
        scratch_shapes=[
            pltpu.SMEM((windows,), jnp.int32),
            pltpu.SMEM((windows,), jnp.int32),
            pltpu.VMEM(norm_gain.shape, BF16),
            pltpu.VMEM(conv_query.shape, BF16),
            pltpu.VMEM(conv_key.shape, BF16),
            pltpu.VMEM(conv_value.shape, BF16),
            pltpu.VMEM(value_gain.shape, BF16),
            dma((8,)),
            pltpu.VMEM((width, half + CHUNK), BF16),
            pltpu.VMEM((half, width), BF16),
            pltpu.VMEM((2, rows_n, half), BF16),
            pltpu.VMEM((rows_n, width), BF16),
            pltpu.VMEM((windows, span + 8, half + CHUNK), F32),
            pltpu.VMEM((windows, span, 3 * HD), BF16),
            pltpu.VMEM((windows, span, 3 * HD), BF16),
            pltpu.VMEM((windows, heads, 2 * FD, span), F32),
            pltpu.VMEM((windows, heads, 2 * FD, span), F32),
            pltpu.VMEM((windows, span, half), BF16),
            pltpu.VMEM((heads, windows, FROWS, HD), F32),
            pltpu.VMEM((heads, windows, FROWS, HD), BF16),
            pltpu.VMEM((heads, windows, FROWS, HD), BF16),
            pltpu.VMEM((windows, span, half), F32),
            pltpu.VMEM((rows_n, half), BF16),
            pltpu.VMEM((vchunks, rows_n, CHUNK), F32),
            pltpu.VMEM((vchunks, rows_n, CHUNK), F32),
            pltpu.VMEM((heads // 2, windows, FROWS, HD), BF16),
            dma((heads // 2,)),
            dma((heads // 2,)),
            dma((3 + vchunks,)),
            dma((vchunks,)),
            dma((vchunks,)),
            dma((vchunks,)),
            dma((vchunks,)),
            dma((vchunks + 1,)),
            dma((vchunks + 1,)),
            dma((heads,)),
            dma((heads,)),
            dma((vchunks,)),
            dma((vchunks,)),
        ],
        compiler_params=pltpu.CompilerParams(
            collective_id=0, has_side_effects=True, vmem_limit_bytes=60 * 1024 * 1024
        ),
        name="layers",
    )(
        doc_start, pad_length, tokens.reshape(rows_n, half), norm_gain, w_query, w_key, w_value,
        conv_query, conv_key, conv_value, value_gain, w_out,
    )
    return out.reshape(1, windows, span, half)


def solution(mesh):
    return jax.shard_map(
        local,
        mesh=mesh,
        in_specs=(
            P("groups", "ctx", "head"),
            P("section", None),
            P("section", None, "head"),
            P("section", None, "head"),
            P("section", None, "head"),
            P("section", None, "head"),
            P("section", None, "head"),
            P("section", None, "head"),
            P("section", "head"),
            P("section", "head", None),
            P("groups"),
            P("groups"),
        ),
        out_specs=P("section", "groups", "ctx", "head"),
        check_vma=False,
    )
```
